512 devices in a mesh: layer: 16 (over z_hi, y), latent: 32 (over z_lo, x, core).
Axes of the slice: x: 4, y: 4, z: 16 (z_hi: 4, z_lo: 4; z = z_hi * 4 + z_lo), core: 2. Of those that a mesh axis runs over, the one named last changes fastest.
Arguments:
- acts: bfloat16 [512, 16, 2304], P('latent', 'layer'), may hold values from -6 to 6
- enc_weight: bfloat16 [16, 2304, 16384], P('layer', None, 'latent'), may hold values from -0.03125 to 0.03125
- enc_bias: float32 [16384], P('latent'), may hold values from -3 to 3
- dec_weight: bfloat16 [16, 16384, 2304], P('layer', 'latent'), may hold values from -0.0625 to 0.0625
- dec_bias: float32 [16, 2304], P('layer'), may hold values from -4 to 4
Outputs:
- recon: bfloat16 [512, 16, 2304], P('latent', 'layer')
The draws below stay inside these ranges and needn't reach their ends.
All inputs are finite; a program needn't handle non-finite values.
Results may differ from the reference program's by a relative error of at most 0.023.
Values may be sent and summed in bfloat16 or wider, within the bound.
A program may use at most 64 MiB of HBM per device.

```python
import jax
import jax.numpy as jnp
from jax import lax

D = 2304
LAT_DEV = 512
LAYERS = 16
LATENTS = 16384
TOKENS = 512
N_LATENT = 32


def levels(own_key, shape, cuts, smallest, high):
    level, own = 1.0, jax.random.fold_in(own_key, 6)
    for axis_at, parts in cuts:
        steps = jnp.exp(jax.random.uniform(jax.random.fold_in(own, axis_at), (parts,), jnp.float32, smallest / len(cuts), high / len(cuts)))
        level = level * jnp.repeat(steps, shape[axis_at] // parts).reshape([-1 if axis == axis_at else 1 for axis in range(len(shape))])
    return level


def scatter_about(key, extent, spread, limit, cuts=(), held_as=jnp.bfloat16):
    array = spread * jax.random.normal(key, extent, jnp.float32)
    if cuts:
        array = array * levels(key, extent, cuts, -0.22, 0.18)
    return jnp.clip(array, -limit, limit).astype(held_as)


def setup_inputs(seed: int = 0) -> dict:
    streams_of = jax.random.split(jax.random.key(seed), 6)
    return {
        "acts": scatter_about(streams_of[0], (TOKENS, LAYERS, D), 1.0, 6.0, ((0, 32), (1, 16))),
        "enc_weight": scatter_about(streams_of[1], (LAYERS, D, LATENTS), (LAYERS * D) ** -0.5, 0.03125, ((0, 16), (2, 32))),
        "enc_bias": scatter_about(streams_of[2], (LATENTS,), 0.5, 3.0, ((0, 32),), jnp.float32),
        "dec_weight": scatter_about(streams_of[3], (LAYERS, LATENTS, D), (LATENTS // 2) ** -0.5, 0.0625, ((0, 16), (1, 32))),
        "dec_bias": scatter_about(streams_of[4], (LAYERS, D), 1.0, 4.0, ((0, 16),), jnp.float32),
    }


def reference(acts, enc_weight, enc_bias, dec_weight, dec_bias):
    def encode_layer(carry, pair):
        rows, weight = pair
        return carry + jnp.dot(rows, weight, preferred_element_type=jnp.float32), None

    start = jnp.zeros((TOKENS, LATENTS), jnp.float32)
    pre, _ = lax.scan(encode_layer, start, (jnp.transpose(acts, (1, 0, 2)), enc_weight))
    codes = jnp.maximum(pre + enc_bias[None, :], 0.0).astype(jnp.bfloat16)
    code_panels = jnp.transpose(codes.reshape(TOKENS, N_LATENT, LAT_DEV), (1, 0, 2))
    dec_panels = jnp.transpose(dec_weight.reshape(LAYERS, N_LATENT, LAT_DEV, D), (1, 0, 2, 3))

    def decode_panel(carry, pair):
        panel_codes, panel_weight = pair
        term = jnp.einsum("tk,lkd->tld", panel_codes.astype(jnp.float32), panel_weight.astype(jnp.float32))
        return carry + term.astype(jnp.bfloat16).astype(jnp.float32), None

    total, _ = lax.scan(decode_panel, jnp.zeros((TOKENS, LAYERS, D), jnp.float32), (code_panels, dec_panels))
    return (total + dec_bias[None, :, :]).astype(jnp.bfloat16)
```

```python
import jax
import jax.numpy as jnp
from jax import lax
from jax.experimental import pallas as pl
from jax.experimental.pallas import tpu as pltpu
from jax.sharding import PartitionSpec as P

MESH = pl.DeviceIdType.MESH
BF, F32 = jnp.bfloat16, jnp.float32
K = 4
ORDER = (
    "A0", "A1", "Y0", "A2", "B0", "C0", "A3", "B1", "C1", "Z0", "D0", "B2", "C2", "D1", "B3", "C3", "E0",
    "D2", "E1", "D3", "F0", "E2", "F1", "E3", "G0", "F2", "H0", "G1", "F3", "H1", "G2", "I0", "H2", "G3",
    "I1", "H3", "I2", "I3",
)


def kernel(
    acts, wenc, benc, wdec, bdec, out,
    xg, we, wd, be, bd, pre, ps, yr, s1, zs, zr, cod, pb, sr, qb, xr, rb, fr, acc,
    local, known, az_s, az_r, ax_s, ax_r, ac_s, ac_r, y_s, y_r, z_s, z_r, yg_s, yg_r,
    c_s, c_r, x_s, x_r, f_s, f_r,
):
    layer, latent = lax.axis_index("layer"), lax.axis_index("latent")
    zh, y = lax.div(layer, 4), lax.rem(layer, 4)
    zl, x, c = lax.div(latent, 8), lax.rem(lax.div(latent, 2), 4), lax.rem(latent, 2)

    def up(v, n):
        return lax.rem(v + n, 4)

    def at(zh_=zh, y_=y, zl_=zl, x_=x, c_=c):
        return {"layer": zh_ * 4 + y_, "latent": (zl_ * 4 + x_) * 2 + c_}

    def along_z(n):
        z = lax.rem(zh * 4 + zl + 16 + n, 16)
        return at(zh_=lax.div(z, 4), zl_=lax.rem(z, 4))

    shifts = (1, 3, 2)
    sib = at(c_=1 - c)
    xs = [up(x, n) for n in shifts]
    ys = [up(y, n) for n in shifts]
    lows = [zl, zl + 1 - 2 * lax.rem(zl, 2), up(zl, 2), 3 - zl]
    inner, outer = zh + 1 - 2 * lax.rem(zh, 2), 3 - zh
    to_x, to_y = [at(x_=v) for v in xs], [at(y_=v) for v in ys]
    to_pair = [at(zh_=inner + c * (outer - inner)), at(zh_=outer + c * (inner - outer))]
    to_zl = [None] + [at(zl_=v) for v in lows[1:]]

    loads = [
        pltpu.make_async_copy(src, dst, local.at[i])
        for i, (src, dst) in enumerate(
            ((acts, xg.at[0, c, x]), (wenc, we), (wdec, wd), (benc, be), (bdec, bd))
        )
    ]
    for load in loads:
        load.start()

    barrier = pltpu.get_barrier_semaphore()
    partners = [sib, *to_x, *to_y, *to_zl[1:], along_z(1), along_z(-1)]
    for partner in partners:
        pl.semaphore_signal(barrier, inc=1, device_id=partner, device_id_type=MESH)
    pl.semaphore_wait(barrier, len(partners))

    def tell(n):
        for partner in (along_z(n), along_z(-n)):
            pl.semaphore_signal(
                known.at[n - 1], inc=1, device_id=partner, device_id_type=MESH
            )

    tell(1)

    sent = []

    def send(src, dst, send_sem, recv_sem, device):
        copy = pltpu.make_async_remote_copy(
            src_ref=src, dst_ref=dst, send_sem=send_sem, recv_sem=recv_sem,
            device_id=device, device_id_type=MESH,
        )
        copy.start()
        sent.append(copy)
        return copy

    az, ax, ac, yy, zz, yg, cc, xx, ff = ({} for _ in range(9))

    def share(k, j, source):
        block = xg.at[k, c, source]
        ac[k, j] = send(block, block, ac_s.at[k, j], ac_r.at[k, j], sib)

    def stage_a(k):
        if k:
            az[k].wait_recv()
        block = xg.at[k, c, x]
        for j in range(3):
            ax[k, j] = send(block, block, ax_s.at[k, j], ax_r.at[k, j], to_x[j])
        if k == 0:
            for i in range(1, K):
                az[i] = send(block, xg.at[i, c, x], az_s.at[i], az_r.at[i], to_zl[i])
        share(k, 3, x)

    def stage_b(k):
        for j, source in enumerate((xs[1], xs[0], xs[2])):
            ax[k, j].wait_recv()
            share(k, j, source)

    def stage_y(k):
        pl.semaphore_wait(known.at[0], 2)
        tell(2)

    def stage_z(k):
        pl.semaphore_wait(known.at[1], 2)

    def stage_c(k):
        for j in range(4):
            ac[k, j].wait_recv()
        if k == 0:
            loads[1].wait()
        rows = xg[k].reshape(128, xg.shape[-1])
        value = jnp.dot(rows, we[...], preferred_element_type=F32)
        pre[k] = value.reshape(pre.shape[1:])
        ps[k] = value.reshape(ps.shape[1:]).astype(BF)
        for j in range(3):
            yy[k, j] = send(ps.at[k, ys[j]], yr.at[k, j], y_s.at[k, j], y_r.at[k, j], to_y[j])

    def stage_d(k):
        for j in range(3):
            yy[k, j].wait_recv()
        value = pre[k, y]
        for j in range(3):
            value = value + yr[k, j].astype(F32)
        s1[k] = value
        zs[k, 0] = value.astype(BF)
        zz[k, 0] = send(zs.at[k, 0], zr.at[k, 0], z_s.at[k, 0], z_r.at[k, 0], to_pair[0])

    def stage_e(k):
        zz[k, 0].wait_recv()
        value = s1[k] + zr[k, 0].astype(F32)
        s1[k] = value
        zs[k, 1] = value.astype(BF)
        zz[k, 1] = send(zs.at[k, 1], zr.at[k, 1], z_s.at[k, 1], z_r.at[k, 1], to_pair[1])

    def stage_f(k):
        zz[k, 1].wait_recv()
        if k == 0:
            loads[3].wait()
        value = s1[k] + zr[k, 1].astype(F32) + be[...]
        cod[k, y] = jnp.maximum(value, 0.0).astype(BF)
        piece = cod.at[k, y]
        for j in range(3):
            yg[k, j] = send(piece, piece, yg_s.at[k, j], yg_r.at[k, j], to_y[j])

    def stage_g(k):
        for j in range(3):
            yg[k, j].wait_recv()
        if k == 0:
            loads[2].wait()
        codes = cod[k].reshape(128, cod.shape[-1])
        part = jnp.dot(codes, wd[...], preferred_element_type=F32)
        pb[k] = part.astype(BF).reshape(pb.shape[1:])
        cc[k] = send(pb.at[k, 1 - c], sr.at[k], c_s.at[k], c_r.at[k], sib)

    def stage_h(k):
        cc[k].wait_recv()
        qb[k] = (pb[k, c].astype(F32) + sr[k].astype(F32)).astype(BF)
        for j in range(3):
            xx[k, j] = send(qb.at[k, xs[j]], xr.at[k, j], x_s.at[k, j], x_r.at[k, j], to_x[j])

    def stage_i(k):
        for j in range(3):
            xx[k, j].wait_recv()
        value = qb[k, x].astype(F32)
        for j in range(3):
            value = value + xr[k, j].astype(F32)
        if k == 0:
            acc[...] = value
        else:
            rb[k] = value.astype(BF)
            ff[k] = send(rb.at[k], fr.at[k], f_s.at[k], f_r.at[k], to_zl[k])

    stages = {
        "A": stage_a, "B": stage_b, "C": stage_c, "D": stage_d, "E": stage_e,
        "F": stage_f, "G": stage_g, "H": stage_h, "I": stage_i,
        "Y": stage_y, "Z": stage_z,
    }
    loads[0].wait()
    for step in ORDER:
        stages[step[0]](int(step[1]))

    loads[4].wait()
    value = acc[...] + bd[...]
    for k in range(1, K):
        ff[k].wait_recv()
        value = value + fr[k].astype(F32)
    out[...] = value.astype(BF)
    for copy in sent:
        copy.wait_send()


def on_device(acts, enc_weight, enc_bias, dec_weight, dec_bias):
    rows, _, width = acts.shape
    panel = enc_weight.shape[2]
    dma = pltpu.SemaphoreType.DMA
    pairs = lambda *shape: [dma(shape), dma(shape)]
    result = pl.pallas_call(
        kernel,
        name="crosscoder",
        out_shape=jax.ShapeDtypeStruct((rows, width), BF),
        in_specs=[pl.BlockSpec(memory_space=pl.ANY)] * 5,
        out_specs=pl.BlockSpec(memory_space=pltpu.VMEM),
        scratch_shapes=[
            pltpu.VMEM((K, 2, 4, rows, width), BF),
            pltpu.VMEM((width, panel), BF),
            pltpu.VMEM((panel, width), BF),
            pltpu.VMEM((1, panel), F32),
            pltpu.VMEM((1, width), F32),
            pltpu.VMEM((K, 4, 32, panel), F32),
            pltpu.VMEM((K, 4, 32, panel), BF),
            pltpu.VMEM((K, 3, 32, panel), BF),
            pltpu.VMEM((K, 32, panel), F32),
            pltpu.VMEM((K, 2, 32, panel), BF),
            pltpu.VMEM((K, 2, 32, panel), BF),
            pltpu.VMEM((K, 4, 32, panel), BF),
            pltpu.VMEM((K, 2, 4, rows, width), BF),
            pltpu.VMEM((K, 4, rows, width), BF),
            pltpu.VMEM((K, 4, rows, width), BF),
            pltpu.VMEM((K, 3, rows, width), BF),
            pltpu.VMEM((K, rows, width), BF),
            pltpu.VMEM((K, rows, width), BF),
            pltpu.VMEM((rows, width), F32),
            dma((5,)),
            pltpu.SemaphoreType.REGULAR((2,)),
            *pairs(K), *pairs(K, 3), *pairs(K, 4), *pairs(K, 3), *pairs(K, 2),
            *pairs(K, 3), *pairs(K), *pairs(K, 3), *pairs(K),
        ],
        compiler_params=pltpu.CompilerParams(collective_id=0, has_side_effects=True),
    )(
        acts.reshape(rows, width),
        enc_weight.reshape(width, panel),
        enc_bias.reshape(1, panel),
        dec_weight.reshape(panel, width),
        dec_bias.reshape(1, width),
    )
    return result.reshape(rows, 1, width)


def solution(mesh):
    return jax.shard_map(
        on_device,
        mesh=mesh,
        in_specs=(
            P("latent", "layer", None),
            P("layer", None, "latent"),
            P("latent"),
            P("layer", "latent", None),
            P("layer", None),
        ),
        out_specs=P("latent", "layer", None),
        check_vma=False,
    )
```

```python
import jax
import jax.numpy as jnp
from jax import lax
from jax.experimental import pallas as pl
from jax.experimental.pallas import tpu as pltpu
from jax.sharding import PartitionSpec as P

MESH = pl.DeviceIdType.MESH
BF, F32 = jnp.bfloat16, jnp.float32
K = 4
ORDER = (
    "A0", "A1", "Y0", "A2", "C0", "A3", "C1", "Z0", "D0", "C2", "D1", "C3", "E0", "D2", "E1", "D3", "F0",
    "E2", "F1", "E3", "G0", "F2", "G1", "F3", "I0", "G2", "I1", "G3", "I2", "I3",
)


def kernel(
    acts, wenc, benc, wdec, bdec, out,
    xg, we, wd, be, bd, pre, ps, yr, s1, zs, zr, cod, qb, xr, rb, fr, acc,
    local, known, w_s, w_r, az_s, az_r, ax_s, ax_r, y_s, y_r, z_s, z_r, yg_s, yg_r,
    x_s, x_r, f_s, f_r,
):
    layer, latent = lax.axis_index("layer"), lax.axis_index("latent")
    half = we.shape[-1]
    zh, y = lax.div(layer, 4), lax.rem(layer, 4)
    zl, x, c = lax.div(latent, 8), lax.rem(lax.div(latent, 2), 4), lax.rem(latent, 2)

    def up(v, n):
        return lax.rem(v + n, 4)

    def at(zh_=zh, y_=y, zl_=zl, x_=x, c_=c):
        return {"layer": zh_ * 4 + y_, "latent": (zl_ * 4 + x_) * 2 + c_}

    def along_z(n):
        z = lax.rem(zh * 4 + zl + 16 + n, 16)
        return at(zh_=lax.div(z, 4), zl_=lax.rem(z, 4))

    shifts = (1, 3, 2)
    sib = at(c_=1 - c)
    xs = [up(x, n) for n in shifts]
    ys = [up(y, n) for n in shifts]
    lows = [zl, zl + 1 - 2 * lax.rem(zl, 2), up(zl, 2), 3 - zl]
    inner, outer = zh + 1 - 2 * lax.rem(zh, 2), 3 - zh
    to_x, to_y = [at(x_=v) for v in xs], [at(y_=v) for v in ys]
    to_pair = [at(zh_=inner + c * (outer - inner)), at(zh_=outer + c * (inner - outer))]
    to_zl = [None] + [at(zl_=v) for v in lows[1:]]

    loads = [
        pltpu.make_async_copy(src, dst, local.at[i])
        for i, (src, dst) in enumerate(
            ((acts, xg.at[0, x]), (wenc, we.at[c]), (wdec, wd.at[c]), (benc, be.at[c]), (bdec, bd))
        )
    ]
    for load in loads:
        load.start()

    barrier = pltpu.get_barrier_semaphore()
    partners = [sib, *to_x, *to_y, *to_zl[1:], along_z(1), along_z(-1)]
    for partner in partners:
        pl.semaphore_signal(barrier, inc=1, device_id=partner, device_id_type=MESH)
    pl.semaphore_wait(barrier, len(partners))

    def tell(n):
        for partner in (along_z(n), along_z(-n)):
            pl.semaphore_signal(
                known.at[n - 1], inc=1, device_id=partner, device_id_type=MESH
            )

    tell(1)

    sent, loaded = [], set()

    def send(src, dst, send_sem, recv_sem, device):
        copy = pltpu.make_async_remote_copy(
            src_ref=src, dst_ref=dst, send_sem=send_sem, recv_sem=recv_sem,
            device_id=device, device_id_type=MESH,
        )
        copy.start()
        sent.append(copy)
        return copy

    ww, az, ax, yy, zz, yg, xx, ff = ({} for _ in range(8))

    def once(i):
        if i not in loaded:
            loaded.add(i)
            loads[i].wait()
            if i in ww:
                ww[i].wait_recv()

    def stage_a(k):
        if k:
            az[k].wait_recv()
        block = xg.at[k, x]
        for j in range(3):
            ax[k, j] = send(block, block, ax_s.at[k, j], ax_r.at[k, j], to_x[j])
        if k == 0:
            for i in range(1, K):
                az[i] = send(block, xg.at[i, x], az_s.at[i], az_r.at[i], to_zl[i])
            for i, src, dst in ((1, wenc, we), (3, benc, be), (2, wdec, wd)):
                ww[i] = send(src, dst.at[c], w_s.at[i], w_r.at[i], sib)

    def stage_y(k):
        pl.semaphore_wait(known.at[0], 2)
        tell(2)

    def stage_z(k):
        pl.semaphore_wait(known.at[1], 2)

    def stage_c(k):
        for j in range(3):
            ax[k, j].wait_recv()
        once(1)
        lines = xg[k].reshape(-1, xg.shape[-1])
        for i in range(2):
            value = jnp.dot(lines, we[i], preferred_element_type=F32)
            value = value.reshape(4, -1, half)
            pre[k, :, :, i * half : (i + 1) * half] = value
            ps[k, :, :, i * half : (i + 1) * half] = value.astype(BF)
        for j in range(3):
            yy[k, j] = send(ps.at[k, ys[j]], yr.at[k, j], y_s.at[k, j], y_r.at[k, j], to_y[j])

    def stage_d(k):
        for j in range(3):
            yy[k, j].wait_recv()
        value = pre[k, y]
        for j in range(3):
            value = value + yr[k, j].astype(F32)
        s1[k] = value
        zs[k, 0] = value.astype(BF)
        zz[k, 0] = send(zs.at[k, 0], zr.at[k, 0], z_s.at[k, 0], z_r.at[k, 0], to_pair[0])

    def stage_e(k):
        zz[k, 0].wait_recv()
        value = s1[k] + zr[k, 0].astype(F32)
        s1[k] = value
        zs[k, 1] = value.astype(BF)
        zz[k, 1] = send(zs.at[k, 1], zr.at[k, 1], z_s.at[k, 1], z_r.at[k, 1], to_pair[1])

    def stage_f(k):
        zz[k, 1].wait_recv()
        once(3)
        bias = jnp.concatenate([be[0], be[1]], axis=1)
        value = s1[k] + zr[k, 1].astype(F32) + bias
        cod[k, y] = jnp.maximum(value, 0.0).astype(BF)
        piece = cod.at[k, y]
        for j in range(3):
            yg[k, j] = send(piece, piece, yg_s.at[k, j], yg_r.at[k, j], to_y[j])

    def stage_g(k):
        for j in range(3):
            yg[k, j].wait_recv()
        once(2)
        codes = cod[k].reshape(-1, 2 * half)
        part = jnp.dot(codes[:, :half], wd[0], preferred_element_type=F32)
        part = part + jnp.dot(codes[:, half:], wd[1], preferred_element_type=F32)
        qb[k] = part.astype(BF).reshape(qb.shape[1:])
        for j in (2, 0, 1):
            xx[k, j] = send(qb.at[k, xs[j]], xr.at[k, j], x_s.at[k, j], x_r.at[k, j], to_x[j])

    def stage_i(k):
        for j in range(3):
            xx[k, j].wait_recv()
        value = qb[k, x].astype(F32)
        for j in range(3):
            value = value + xr[k, j].astype(F32)
        if k == 0:
            acc[...] = value
        else:
            rb[k] = value.astype(BF)
            ff[k] = send(rb.at[k], fr.at[k], f_s.at[k], f_r.at[k], to_zl[k])

    stages = {
        "A": stage_a, "C": stage_c, "D": stage_d, "E": stage_e,
        "F": stage_f, "G": stage_g, "I": stage_i, "Y": stage_y, "Z": stage_z,
    }
    once(0)
    for step in ORDER:
        stages[step[0]](int(step[1]))

    once(4)
    value = acc[...] + bd[...]
    for k in range(1, K):
        ff[k].wait_recv()
        value = value + fr[k].astype(F32)
    out[...] = value.astype(BF)
    for copy in sent:
        copy.wait_send()


def on_device(acts, enc_weight, enc_bias, dec_weight, dec_bias):
    rows, _, width = acts.shape
    panel = enc_weight.shape[2]
    dma = pltpu.SemaphoreType.DMA
    pairs = lambda *shape: [dma(shape), dma(shape)]
    result = pl.pallas_call(
        kernel,
        name="crosscoder",
        out_shape=jax.ShapeDtypeStruct((rows, width), BF),
        in_specs=[pl.BlockSpec(memory_space=pl.ANY)] * 5,
        out_specs=pl.BlockSpec(memory_space=pltpu.VMEM),
        scratch_shapes=[
            pltpu.VMEM((K, 4, rows, width), BF),
            pltpu.VMEM((2, width, panel), BF),
            pltpu.VMEM((2, panel, width), BF),
            pltpu.VMEM((2, 1, panel), F32),
            pltpu.VMEM((1, width), F32),
            pltpu.VMEM((K, 4, rows, 2 * panel), F32),
            pltpu.VMEM((K, 4, rows, 2 * panel), BF),
            pltpu.VMEM((K, 3, rows, 2 * panel), BF),
            pltpu.VMEM((K, rows, 2 * panel), F32),
            pltpu.VMEM((K, 2, rows, 2 * panel), BF),
            pltpu.VMEM((K, 2, rows, 2 * panel), BF),
            pltpu.VMEM((K, 4, rows, 2 * panel), BF),
            pltpu.VMEM((K, 4, rows, width), BF),
            pltpu.VMEM((K, 3, rows, width), BF),
            pltpu.VMEM((K, rows, width), BF),
            pltpu.VMEM((K, rows, width), BF),
            pltpu.VMEM((rows, width), F32),
            dma((5,)),
            pltpu.SemaphoreType.REGULAR((2,)),
            *pairs(K), *pairs(K), *pairs(K, 3), *pairs(K, 3), *pairs(K, 2),
            *pairs(K, 3), *pairs(K, 3), *pairs(K),
        ],
        compiler_params=pltpu.CompilerParams(collective_id=0, has_side_effects=True),
    )(
        acts.reshape(rows, width),
        enc_weight.reshape(width, panel),
        enc_bias.reshape(1, panel),
        dec_weight.reshape(panel, width),
        dec_bias.reshape(1, width),
    )
    return result.reshape(rows, 1, width)


def solution(mesh):
    return jax.shard_map(
        on_device,
        mesh=mesh,
        in_specs=(
            P("latent", "layer", None),
            P("layer", None, "latent"),
            P("latent"),
            P("layer", "latent", None),
            P("layer", None),
        ),
        out_specs=P("latent", "layer", None),
        check_vma=False,
    )
```

```python
import jax
import jax.numpy as jnp
from jax import lax
from jax.experimental import pallas as pl
from jax.experimental.pallas import tpu as pltpu
from jax.sharding import PartitionSpec as P

MESH = pl.DeviceIdType.MESH
BF, F32 = jnp.bfloat16, jnp.float32
K = 4
ORDER = (
    "A0", "A1", "Y0", "A2", "C0", "A3", "C1", "Z0", "D0", "C2", "D1", "C3", "E0", "D2", "E1", "D3", "F0",
    "E2", "F1", "E3", "G0", "F2", "G1", "F3", "I0", "G2", "I1", "G3", "I2", "I3",
)


def kernel(
    acts, wenc, benc, wdec, bdec, out,
    xg, we, wd, be, bd, pre, ps, yr, s1, zs, zr, cod, qb, xr, rb, fr, acc,
    local, known, w_s, w_r, az_s, az_r, ax_s, ax_r, y_s, y_r, z_s, z_r, yg_s, yg_r,
    x_s, x_r, f_s, f_r,
):
    layer, latent = lax.axis_index("layer"), lax.axis_index("latent")
    half = we.shape[-1]
    zh, y = lax.div(layer, 4), lax.rem(layer, 4)
    zl, x, c = lax.div(latent, 8), lax.rem(lax.div(latent, 2), 4), lax.rem(latent, 2)

    def up(v, n):
        return lax.rem(v + n, 4)

    def at(zh_=zh, y_=y, zl_=zl, x_=x, c_=c):
        return {"layer": zh_ * 4 + y_, "latent": (zl_ * 4 + x_) * 2 + c_}

    def along_z(n):
        z = lax.rem(zh * 4 + zl + 16 + n, 16)
        return at(zh_=lax.div(z, 4), zl_=lax.rem(z, 4))

    shifts = (1, 3, 2)
    sib = at(c_=1 - c)
    xs = [up(x, n) for n in shifts]
    ys = [up(y, n) for n in shifts]
    lows = [zl, zl + 1 - 2 * lax.rem(zl, 2), up(zl, 2), 3 - zl]
    inner, outer = zh + 1 - 2 * lax.rem(zh, 2), 3 - zh
    to_x, to_y = [at(x_=v) for v in xs], [at(y_=v) for v in ys]
    to_pair = [at(zh_=inner + c * (outer - inner)), at(zh_=outer + c * (inner - outer))]
    to_zl = [None] + [at(zl_=v) for v in lows[1:]]

    loads = [
        pltpu.make_async_copy(src, dst, local.at[i])
        for i, (src, dst) in enumerate(
            ((acts, xg.at[0, x]), (wenc, we.at[c]), (wdec, wd.at[c]), (benc, be.at[c]), (bdec, bd))
        )
    ]
    for load in loads:
        load.start()

    barrier = pltpu.get_barrier_semaphore()
    partners = [sib, *to_x, *to_y, *to_zl[1:], along_z(1), along_z(-1)]
    for partner in partners:
        pl.semaphore_signal(barrier, inc=1, device_id=partner, device_id_type=MESH)
    pl.semaphore_wait(barrier, len(partners))

    def tell(n):
        for partner in (along_z(n), along_z(-n)):
            pl.semaphore_signal(
                known.at[n - 1], inc=1, device_id=partner, device_id_type=MESH
            )

    tell(1)

    sent, loaded = [], set()

    def send(src, dst, send_sem, recv_sem, device):
        copy = pltpu.make_async_remote_copy(
            src_ref=src, dst_ref=dst, send_sem=send_sem, recv_sem=recv_sem,
            device_id=device, device_id_type=MESH,
        )
        copy.start()
        sent.append(copy)
        return copy

    ww, az, ax, yy, zz, yg, xx, ff = ({} for _ in range(8))

    def once(i):
        if i not in loaded:
            loaded.add(i)
            loads[i].wait()
            if i in ww:
                ww[i].wait_recv()

    def stage_a(k):
        if k:
            az[k].wait_recv()
        block = xg.at[k, x]
        for j in (2, 0, 1):
            ax[k, j] = send(block, block, ax_s.at[k, j], ax_r.at[k, j], to_x[j])
        if k == 0:
            for i in range(1, K):
                az[i] = send(block, xg.at[i, x], az_s.at[i], az_r.at[i], to_zl[i])
            for i, src, dst in ((1, wenc, we), (3, benc, be), (2, wdec, wd)):
                ww[i] = send(src, dst.at[c], w_s.at[i], w_r.at[i], sib)

    def stage_y(k):
        pl.semaphore_wait(known.at[0], 2)
        tell(2)

    def stage_z(k):
        pl.semaphore_wait(known.at[1], 2)

    def stage_c(k):
        for j in range(3):
            ax[k, j].wait_recv()
        once(1)
        lines = xg[k].reshape(-1, xg.shape[-1])
        for i in range(2):
            value = jnp.dot(lines, we[i], preferred_element_type=F32)
            value = value.reshape(4, -1, half)
            pre[k, :, :, i * half : (i + 1) * half] = value
            ps[k, :, :, i * half : (i + 1) * half] = value.astype(BF)
        for j in (2, 0, 1):
            yy[k, j] = send(ps.at[k, ys[j]], yr.at[k, j], y_s.at[k, j], y_r.at[k, j], to_y[j])

    def stage_d(k):
        for j in range(3):
            yy[k, j].wait_recv()
        value = pre[k, y]
        for j in range(3):
            value = value + yr[k, j].astype(F32)
        s1[k] = value
        zs[k, 0] = value.astype(BF)
        zz[k, 0] = send(zs.at[k, 0], zr.at[k, 0], z_s.at[k, 0], z_r.at[k, 0], to_pair[0])

    def stage_e(k):
        zz[k, 0].wait_recv()
        value = s1[k] + zr[k, 0].astype(F32)
        s1[k] = value
        zs[k, 1] = value.astype(BF)
        zz[k, 1] = send(zs.at[k, 1], zr.at[k, 1], z_s.at[k, 1], z_r.at[k, 1], to_pair[1])

    def stage_f(k):
        zz[k, 1].wait_recv()
        once(3)
        bias = jnp.concatenate([be[0], be[1]], axis=1)
        value = s1[k] + zr[k, 1].astype(F32) + bias
        cod[k, y] = jnp.maximum(value, 0.0).astype(BF)
        piece = cod.at[k, y]
        for j in (2, 0, 1):
            yg[k, j] = send(piece, piece, yg_s.at[k, j], yg_r.at[k, j], to_y[j])

    def stage_g(k):
        for j in range(3):
            yg[k, j].wait_recv()
        once(2)
        codes = cod[k].reshape(-1, 2 * half)
        part = jnp.dot(codes[:, :half], wd[0], preferred_element_type=F32)
        part = part + jnp.dot(codes[:, half:], wd[1], preferred_element_type=F32)
        qb[k] = part.astype(BF).reshape(qb.shape[1:])
        for j in (2, 0, 1):
            xx[k, j] = send(qb.at[k, xs[j]], xr.at[k, j], x_s.at[k, j], x_r.at[k, j], to_x[j])

    def stage_i(k):
        for j in range(3):
            xx[k, j].wait_recv()
        value = qb[k, x].astype(F32)
        for j in range(3):
            value = value + xr[k, j].astype(F32)
        if k == 0:
            acc[...] = value
        else:
            rb[k] = value.astype(BF)
            ff[k] = send(rb.at[k], fr.at[k], f_s.at[k], f_r.at[k], to_zl[k])

    stages = {
        "A": stage_a, "C": stage_c, "D": stage_d, "E": stage_e,
        "F": stage_f, "G": stage_g, "I": stage_i, "Y": stage_y, "Z": stage_z,
    }
    once(0)
    for step in ORDER:
        stages[step[0]](int(step[1]))

    once(4)
    value = acc[...] + bd[...]
    for k in range(1, K):
        ff[k].wait_recv()
        value = value + fr[k].astype(F32)
    out[...] = value.astype(BF)
    for copy in sent:
        copy.wait_send()


def on_device(acts, enc_weight, enc_bias, dec_weight, dec_bias):
    rows, _, width = acts.shape
    panel = enc_weight.shape[2]
    dma = pltpu.SemaphoreType.DMA
    pairs = lambda *shape: [dma(shape), dma(shape)]
    held = lambda v: pltpu.with_memory_space_constraint(v, pltpu.HBM)
    result = pl.pallas_call(
        kernel,
        name="crosscoder",
        out_shape=jax.ShapeDtypeStruct((rows, width), BF),
        in_specs=[pl.BlockSpec(memory_space=pl.ANY)] * 5,
        out_specs=pl.BlockSpec(memory_space=pltpu.VMEM),
        scratch_shapes=[
            pltpu.VMEM((K, 4, rows, width), BF),
            pltpu.VMEM((2, width, panel), BF),
            pltpu.VMEM((2, panel, width), BF),
            pltpu.VMEM((2, 1, panel), F32),
            pltpu.VMEM((1, width), F32),
            pltpu.VMEM((K, 4, rows, 2 * panel), F32),
            pltpu.VMEM((K, 4, rows, 2 * panel), BF),
            pltpu.VMEM((K, 3, rows, 2 * panel), BF),
            pltpu.VMEM((K, rows, 2 * panel), F32),
            pltpu.VMEM((K, 2, rows, 2 * panel), BF),
            pltpu.VMEM((K, 2, rows, 2 * panel), BF),
            pltpu.VMEM((K, 4, rows, 2 * panel), BF),
            pltpu.VMEM((K, 4, rows, width), BF),
            pltpu.VMEM((K, 3, rows, width), BF),
            pltpu.VMEM((K, rows, width), BF),
            pltpu.VMEM((K, rows, width), BF),
            pltpu.VMEM((rows, width), F32),
            dma((5,)),
            pltpu.SemaphoreType.REGULAR((2,)),
            *pairs(K), *pairs(K), *pairs(K, 3), *pairs(K, 3), *pairs(K, 2),
            *pairs(K, 3), *pairs(K, 3), *pairs(K),
        ],
        compiler_params=pltpu.CompilerParams(collective_id=0, has_side_effects=True, vmem_limit_bytes=48*1024*1024),
    )(
        held(acts.reshape(rows, width)),
        held(enc_weight.reshape(width, panel)),
        held(enc_bias.reshape(1, panel)),
        held(dec_weight.reshape(panel, width)),
        held(dec_bias.reshape(1, width)),
    )
    return result.reshape(rows, 1, width)


def solution(mesh):
    return jax.shard_map(
        on_device,
        mesh=mesh,
        in_specs=(
            P("latent", "layer", None),
            P("layer", None, "latent"),
            P("latent"),
            P("layer", "latent", None),
            P("layer", None),
        ),
        out_specs=P("latent", "layer", None),
        check_vma=False,
    )
```
